32 devices in a mesh: pipe: 4 (over y, core), expert: 8 (over z, x).
Axes of the slice: x: 2, y: 2, z: 4, core: 2. Of those that a mesh axis runs over, the one named last changes fastest.
Arguments:
- tokens: bfloat16 [4, 1024, 2048], P('pipe', 'expert'), may hold values from -6 to 6
- out_grad: bfloat16 [4, 1024, 2048], P('pipe', 'expert'), may hold values from -6 to 6
- gates: float32 [4, 1024, 2], P('pipe', 'expert'), may hold values from 0.1 to 1
- expert_ids: int32 [4, 1024, 2], P('pipe', 'expert'), may hold values from 0 to 7, all different within a row; in each aligned block of 128 rows (0 to 127, 128 to 255, ..., all dimensions but the last counted through in order) at most 64 rows name the same one
- w_gate: bfloat16 [4, 8, 2048, 768], P('pipe', 'expert'), may hold values from -0.125 to 0.125
- w_up: bfloat16 [4, 8, 2048, 768], P('pipe', 'expert'), may hold values from -0.125 to 0.125
- w_down: bfloat16 [4, 8, 768, 2048], P('pipe', 'expert'), may hold values from -0.21875 to 0.21875
Outputs:
- arrived: bfloat16 [4, 1024, 2048], P('pipe', 'expert')
- grad_gates: bfloat16 [4, 1024, 2], P('pipe', 'expert')
The draws below stay inside these ranges and needn't reach their ends.
Inputs may be any that keep to these rules, and one draw needn't show every extreme that they name: `expert_ids`: the 2 ids of a token differ. In each aligned block of 128 rows of a section (the tokens of one device) no expert is named by more than 64 rows, a bound that some block reaches.
All inputs are finite; a program needn't handle non-finite values.
Results may differ from the reference program's by a relative error of at most 0.0057.
Values may be sent and summed in bfloat16 or wider, within the bound.
A program may use at most 64 MiB of HBM per device.

```python
import math
import jax
import jax.numpy as jnp
import numpy as np
from jax import lax

D = 2048
FF = 768
TOP = 2
TOK_DEV = 128
EXPERTS = 8
TOKENS = 1024
CAP = 64
PIPE = 4
N_EXPERT = 8


def shard_levels(own_key, shape, split, smallest, high):
    loudness = 1.0
    for position, shards_of in split:
        steps = jax.random.uniform(jax.random.fold_in(jax.random.fold_in(own_key, 6), position), (shards_of,), jnp.float32, smallest / len(split), high / len(split))
        loudness = loudness * jnp.repeat(jnp.exp(steps), shape[position] // shards_of).reshape((-1,) + (1,) * (len(shape) - 1 - position))
    return loudness


def routed_block(stream_key, own, number, rows, count, top, bound, slope):
    ranking = jax.random.permutation(stream_key, count)
    packed, common = shares(count, rows * top, bound, slope, True), shares(count, rows * top, bound, slope, False)
    places = jnp.arange(count)

    def named(lengths, rotation):
        used = int((lengths > 0).sum())
        fixed = max(1, used // 4)
        moved = fixed + (places - fixed + rotation * (used - fixed)) % max(1, count - fixed)
        return jnp.zeros((count,), jnp.int32).at[ranking[jnp.where(places < fixed, places, moved)]].set(jnp.asarray(lengths, jnp.int32))

    lengths = jnp.where(number % 4 == 0, named(packed, number // 4), named(common, number - number // 4 - 1))
    mixed = jax.random.permutation(jax.random.fold_in(own, 3), count)
    giver, taker = mixed[0:count // 2 * 2:2], mixed[1:count // 2 * 2:2]
    margin = jnp.minimum(lengths[giver] - 1, bound - lengths[taker]) // 2
    margin = jnp.where((giver == ranking[0]) | (taker == ranking[0]) | (lengths[taker] == 0), 0, jnp.maximum(margin, 0))
    moved = jax.random.randint(jax.random.fold_in(own, 4), (count // 2,), 0, 1 << 20) % (margin + 1)
    lengths = lengths.at[giver].add(-moved).at[taker].add(moved)
    items = jnp.searchsorted(jnp.cumsum(lengths), jnp.arange(rows * top), side="right").astype(jnp.int32)
    listing = items.reshape(top, rows).T
    listing = listing[jax.random.permutation(jax.random.fold_in(own, 1), rows)]
    rotation = jax.random.randint(jax.random.fold_in(own, 2), (rows, 1), 0, top)
    return jnp.take_along_axis(listing, (jnp.arange(top)[None, :] + rotation) % top, axis=1)


def shares(count, total, most, slope, full):
    loads = [(1 << 20) // math.isqrt(standing ** slope) + 1 for standing in range(1, count + 1)]
    largest = most if full else min(most, max(-(-total // count), total * loads[0] // sum(loads)))
    least = 1 if total - largest >= count - 1 else 0
    holding, surplus = [largest] + [least] * (count - 1), total - largest - least * (count - 1)
    while surplus > 0:
        free = [i for i in range(1, count) if holding[i] < largest] or [i for i in range(1, count) if holding[i] < most]
        whole, left = sum([loads[i] for i in free]), surplus
        for i in free:
            more = min(most - holding[i], max(1, left * loads[i] // whole), surplus)
            holding[i] = holding[i] + more
            surplus = surplus - more
    return np.array(holding)


def gaussian(rng, dims, scale, reach, cuts=(), kind=jnp.bfloat16):
    gain = shard_levels(rng, dims, cuts, -0.22, 0.18) if cuts else 1.0
    entries = jax.random.normal(rng, dims, jnp.float32) * scale * gain
    return jnp.minimum(jnp.maximum(entries, -reach), reach).astype(kind)


def setup_inputs(seed: int = 0) -> dict:
    streams_of = jax.random.split(jax.random.key(seed), 8)
    tokens = gaussian(streams_of[0], (PIPE, TOKENS, D), 1.0, 6.0, ((0, 4), (1, 8)))
    out_grad = gaussian(streams_of[1], (PIPE, TOKENS, D), 1.0, 6.0, ((0, 4), (1, 8)))
    gates = jnp.clip(0.1 + 0.9 * jax.random.uniform(streams_of[2], (PIPE, TOKENS, TOP), jnp.float32) ** shard_levels(streams_of[2], (PIPE, TOKENS, TOP), ((0, 4), (1, 8)), -0.2, 0.2), 0.1, 1.0)
    expert_ids_keys = jax.random.split(jax.random.fold_in(streams_of[3], 1), PIPE * TOKENS // TOK_DEV)
    expert_ids_turns = jax.random.permutation(jax.random.fold_in(streams_of[3], 3), PIPE * TOKENS // TOK_DEV)
    expert_ids = jax.vmap(lambda own, number: routed_block(jax.random.fold_in(streams_of[3], 2), own, number, TOK_DEV, EXPERTS, TOP, CAP, 2))(expert_ids_keys, expert_ids_turns).reshape((PIPE, TOKENS, TOP))
    w_gate = gaussian(streams_of[4], (PIPE, EXPERTS, D, FF), D ** -0.5, 0.125, ((0, 4), (1, 8)))
    w_up = gaussian(streams_of[5], (PIPE, EXPERTS, D, FF), D ** -0.5, 0.125, ((0, 4), (1, 8)))
    w_down = gaussian(streams_of[6], (PIPE, EXPERTS, FF, D), FF ** -0.5, 0.21875, ((0, 4), (1, 8)))
    return {"tokens": tokens, "out_grad": out_grad, "gates": gates, "expert_ids": expert_ids, "w_gate": w_gate, "w_up": w_up, "w_down": w_down}


def expert_backward(rows, row_grads, gate_weight, up_weight, down_weight):
    gate = jnp.dot(rows, gate_weight, preferred_element_type=jnp.float32)
    up_proj = jnp.dot(rows, up_weight, preferred_element_type=jnp.float32)
    sigmoid_gate = jax.nn.sigmoid(gate)
    activated = gate * sigmoid_gate
    hidden = activated * up_proj
    d_hidden = jnp.dot(row_grads, down_weight.T, preferred_element_type=jnp.float32)
    gate_grad = jnp.sum(d_hidden * hidden, axis=-1).astype(jnp.bfloat16)
    d_up = (d_hidden * activated).astype(jnp.bfloat16)
    d_gate = (d_hidden * up_proj * sigmoid_gate * (1.0 + gate * (1.0 - sigmoid_gate))).astype(jnp.bfloat16)
    route_grad = jnp.dot(d_gate, gate_weight.T, preferred_element_type=jnp.float32)
    route_grad = route_grad + jnp.dot(d_up, up_weight.T, preferred_element_type=jnp.float32)
    return route_grad.astype(jnp.bfloat16), gate_grad


def section_backward(inputs):
    tokens, out_grad, gates, expert_ids, w_gate, w_up, w_down = inputs
    source_ids = expert_ids.reshape(N_EXPERT, TOK_DEV * TOP).astype(jnp.int32)
    one_hot = (source_ids[:, :, None] == jnp.arange(EXPERTS, dtype=jnp.int32)[None, None, :]).astype(jnp.int32)
    route_rank = jnp.cumsum(one_hot, axis=1) - one_hot
    slot_index = jnp.sum(route_rank * one_hot, axis=-1).astype(jnp.int32)
    source_index = jnp.broadcast_to(jnp.arange(N_EXPERT, dtype=jnp.int32)[:, None], source_ids.shape)
    token_index = (source_index * TOK_DEV + jnp.arange(TOK_DEV * TOP, dtype=jnp.int32)[None, :] // TOP).astype(jnp.int32)
    table = jnp.full((EXPERTS, N_EXPERT, CAP), TOKENS, jnp.int32)
    table = table.at[source_ids, source_index, slot_index].set(token_index)
    padded_tokens = jnp.concatenate([tokens, jnp.zeros((1, D), jnp.bfloat16)], axis=0)
    padded_grads = jnp.concatenate([out_grad, jnp.zeros((1, D), jnp.bfloat16)], axis=0)

    def one_expert(pieces):
        row_index, gate_weight, up_weight, down_weight = pieces
        flat_index = row_index.reshape(-1)
        return expert_backward(padded_tokens[flat_index], padded_grads[flat_index], gate_weight, up_weight, down_weight)

    route_grads, gate_grads = lax.map(one_expert, (table, w_gate, w_up, w_down))
    flat_slot = (source_index * CAP + slot_index).astype(jnp.int32)
    picked = route_grads[source_ids, flat_slot].reshape(TOKENS, TOP, D)
    section_grad = jnp.sum(picked.astype(jnp.float32) * gates[:, :, None], axis=1).astype(jnp.bfloat16)
    grad_gates = gate_grads[source_ids, flat_slot].reshape(TOKENS, TOP)
    return section_grad, grad_gates


def reference(tokens, out_grad, gates, expert_ids, w_gate, w_up, w_down):
    section_grads, grad_gates = lax.map(section_backward, (tokens, out_grad, gates, expert_ids, w_gate, w_up, w_down))
    arrived = jnp.concatenate([section_grads[1:], jnp.zeros_like(section_grads[:1])], axis=0)
    return arrived, grad_gates
```

```python
import functools
import jax
import jax.numpy as jnp
from jax import lax
from jax.experimental import pallas as pl
from jax.experimental.pallas import tpu as pltpu
from jax.sharding import PartitionSpec as P

F32 = jnp.float32
BF16 = jnp.bfloat16
CHUNKS = 4


def kernel(
    pipes, zs, xs, cap,
    tok_ref, grad_ref, ids_ref, gates_ref, wg_ref, wu_ref, wd_ref,
    out_ref, gg_ref,
    wg, wu, wd, blk, sel_out, sel_in, gate_s, up_s, dh_s, dgate_s, dup_s, slot_gate,
    ret_out, ret_in, part, chain, stage, meta, ggbuf, ggout,
    w_sem, own_sem, own_send, fwd_send, blk_recv, xs_send, xs_recv, m_send, m_recv,
    g_send, g_recv, xr_send, xr_recv, ch_send, ch_recv, p_send, p_recv,
):
    n = zs * xs
    pipe = lax.axis_index("pipe")
    me = lax.axis_index("expert")
    z, x = me // xs, me % xs
    rows, width = tok_ref.shape
    cols = width // CHUNKS
    slots = xs * cap
    hidden = wg.shape[1]
    htile = 256
    mesh_ids = pl.DeviceIdType.MESH

    def remote(src, dst, ssem, rsem, **dev):
        return pltpu.make_async_remote_copy(
            src_ref=src, dst_ref=dst, send_sem=ssem, recv_sem=rsem,
            device_id=dev, device_id_type=mesh_ids,
        )

    loads = [
        pltpu.make_async_copy(wg_ref, wg, w_sem.at[0]),
        pltpu.make_async_copy(wu_ref, wu, w_sem.at[1]),
        pltpu.make_async_copy(wd_ref, wd, w_sem.at[2]),
    ]
    owns = [
        pltpu.make_async_copy(tok_ref, blk.at[0, z], own_sem.at[0]),
        pltpu.make_async_copy(grad_ref, blk.at[1, z], own_sem.at[1]),
    ]
    for c in owns + loads:
        c.start()

    barrier = pltpu.get_barrier_semaphore()
    prev_pipe = lax.rem(pipe + pipes - 1, pipes)
    next_pipe = lax.rem(pipe + 1, pipes)
    for i in range(1, n):
        pl.semaphore_signal(
            barrier, inc=1, device_id={"expert": lax.rem(me + i, n)}, device_id_type=mesh_ids
        )
    for other in (prev_pipe, next_pipe):
        pl.semaphore_signal(barrier, inc=1, device_id={"pipe": other}, device_id_type=mesh_ids)
    pl.semaphore_wait(barrier, n + 1)

    def own_copy(k, up):
        src = (tok_ref, grad_ref)[k]
        return remote(
            src, blk.at[k, z], own_send.at[up, k], blk_recv.at[k, z],
            expert=me + xs if up else me - xs,
        )

    for k in range(2):
        @pl.when(z < zs - 1)
        def _():
            own_copy(k, 1).start()

        @pl.when(z > 0)
        def _():
            own_copy(k, 0).start()

    ids = ids_ref[...]
    sub = lax.broadcasted_iota(jnp.int32, (n, rows), 0)
    hot0 = (sub == ids[0:1]).astype(F32)
    hot1 = (sub == ids[1:2]).astype(F32)
    before = (
        lax.broadcasted_iota(jnp.int32, (rows, rows), 0)
        < lax.broadcasted_iota(jnp.int32, (rows, rows), 1)
    ).astype(F32).astype(BF16)
    earlier = jnp.dot((hot0 + hot1).astype(BF16), before, preferred_element_type=F32)
    idf = ids.astype(F32) * cap
    pos0 = idf[0:1] + jnp.sum(hot0 * earlier, axis=0, keepdims=True)
    pos1 = idf[1:2] + jnp.sum(hot1 * earlier, axis=0, keepdims=True)
    meta[me, 0:1] = pos0
    meta[me, 1:2] = pos1
    meta[me, 2:4] = gates_ref[...]
    meta[me, 4:8] = jnp.zeros((4, rows), F32)

    def meta_copy(i):
        return remote(
            meta.at[me], meta.at[me], m_send.at[i], m_recv.at[me], expert=lax.rem(me + i, n)
        )

    def meta_wait(i):
        e = lax.rem(me + i, n)
        remote(meta.at[e], meta.at[e], m_send.at[i], m_recv.at[e], expert=e).wait_recv()

    for i in range(1, n):
        meta_copy(i).start()
    for i in range(1, n):
        meta_wait(i)

    def onehot(e, first, count):
        want = (first + lax.broadcasted_iota(jnp.int32, (count, rows), 0)).astype(F32)
        m = meta[e]
        return (want == m[0:1]).astype(F32), (want == m[1:2]).astype(F32), m

    def fwd_copy(k, zp):
        return remote(
            blk.at[k, zp], blk.at[k, zp], fwd_send.at[k, zp], blk_recv.at[k, zp],
            expert=jnp.where(zp > z, me - xs, me + xs),
        )

    def can_fwd(zp):
        return ((zp > z) & (z > 0)) | ((zp < z) & (z < zs - 1))

    def xsel_copy(k, zp, i):
        to = lax.rem(x + i, xs)
        return remote(
            sel_out.at[k, zp, to], sel_in.at[k, zp, x], xs_send.at[k, zp, i],
            xs_recv.at[k, zp, x], expert=z * xs + to,
        )

    def xsel_wait(k, zp, i):
        fr = lax.rem(x + i, xs)
        remote(
            sel_out.at[k, zp, fr], sel_in.at[k, zp, fr], xs_send.at[k, zp, i],
            xs_recv.at[k, zp, fr], expert=z * xs + fr,
        ).wait_recv()

    def xret_copy(zp, c, i):
        to = lax.rem(x + i, xs)
        return remote(
            ret_out.at[zp, c, to], ret_in.at[zp, c, x], xr_send.at[zp, c, i],
            xr_recv.at[zp, c, x], expert=z * xs + to,
        )

    def xret_wait(zp, c, i):
        fr = lax.rem(x + i, xs)
        remote(
            ret_out.at[zp, c, fr], ret_in.at[zp, c, fr], xr_send.at[zp, c, i],
            xr_recv.at[zp, c, fr], expert=z * xs + fr,
        ).wait_recv()

    def chain_copy(zp, c):
        up = (zp > z).astype(jnp.int32)
        return remote(
            part.at[zp, c], chain.at[up, zp, c], ch_send.at[zp, c], ch_recv.at[up, zp, c],
            expert=jnp.where(zp > z, me + xs, me - xs),
        )

    def chain_wait(up, zp, c):
        remote(
            part.at[zp, c], chain.at[up, zp, c], ch_send.at[zp, c], ch_recv.at[up, zp, c],
            expert=jnp.where(up == 1, me - xs, me + xs),
        ).wait_recv()

    def gg_copy(e):
        return remote(ggout.at[e], ggbuf.at[me], g_send.at[e], g_recv.at[me], expert=e)

    def gg_wait(e):
        remote(ggout.at[e], ggbuf.at[e], g_send.at[e], g_recv.at[e], expert=e).wait_recv()

    def take(k, zp, d):
        @pl.when(d > 0)
        def _():
            fwd_copy(k, zp).wait_recv()

            @pl.when(can_fwd(zp))
            def _():
                fwd_copy(k, zp).start()

        o0, o1, _ = onehot(zp * xs + x, z * slots, slots)
        hot = (o0 + o1).astype(BF16)

        def col(c, _):
            at = pl.ds(pl.multiple_of(c * cols, cols), cols)
            got = jnp.dot(hot, blk[k, zp, :, at], preferred_element_type=F32).astype(BF16)
            sel_out[k, zp, :, :, at] = got.reshape(xs, cap, cols)
            return 0

        lax.fori_loop(0, CHUNKS, col, 0)
        for i in range(1, xs):
            xsel_copy(k, zp, i).start()
        sel_in[k, zp, x] = sel_out[k, zp, x]

    def work(zp):
        for k in range(2):
            for i in range(1, xs):
                xsel_wait(k, zp, i)
        contract_last = (((1,), (1,)), ((), ()))

        def tile(h, _):
            at = pl.ds(pl.multiple_of(h * htile, htile), htile)
            a = sel_in[0, zp].reshape(slots, width)
            b = sel_in[1, zp].reshape(slots, width)
            gate = jnp.dot(a, wg[:, at], preferred_element_type=F32)
            up = jnp.dot(a, wu[:, at], preferred_element_type=F32)
            dh = lax.dot_general(b, wd[at, :], contract_last, preferred_element_type=F32)
            sig = jax.nn.sigmoid(gate)
            act = gate * sig
            dup_s[:, at] = (dh * act).astype(BF16)
            dgate_s[:, at] = (dh * up * sig * (1.0 + gate * (1.0 - sig))).astype(BF16)
            return _ + jnp.sum(dh * (act * up), axis=-1, keepdims=True)

        gg = lax.fori_loop(0, hidden // htile, tile, jnp.zeros((slots, 1), F32))
        for s in range(xs):
            e = zp * xs + s
            o0, o1, m = onehot(e, me * cap, cap)
            slot_gate[s * cap:(s + 1) * cap] = jnp.sum(
                o0 * m[2:3] + o1 * m[3:4], axis=1, keepdims=True
            )
            mine = gg[s * cap:(s + 1) * cap]
            ggout[e, 0:1] = jnp.sum(o0 * mine, axis=0, keepdims=True)
            ggout[e, 1:2] = jnp.sum(o1 * mine, axis=0, keepdims=True)

            @pl.when(e != me)
            def _():
                gg_copy(e).start()

        def col(c, _):
            at = pl.ds(pl.multiple_of(c * cols, cols), cols)
            r = lax.dot_general(dgate_s[...], wg[at, :], contract_last, preferred_element_type=F32)
            r = r + lax.dot_general(dup_s[...], wu[at, :], contract_last, preferred_element_type=F32)
            r = (r * slot_gate[...]).astype(BF16)
            ret_out[zp, c] = r.reshape(xs, cap, cols)
            for i in range(1, xs):
                xret_copy(zp, c, i).start()
            ret_in[zp, c, x] = ret_out[zp, c, x]
            return 0

        lax.fori_loop(0, CHUNKS, col, 0)

    def combine(zp):
        o0, o1, _ = onehot(zp * xs + x, z * slots, slots)
        hot = (o0 + o1).astype(BF16)
        head = ((z == 0) & (zp > 0)) | ((z == zs - 1) & (zp < z))

        def col(c, _):
            for i in range(1, xs):
                xret_wait(zp, c, i)
            r = ret_in[zp, c].reshape(slots, cols)
            part[zp, c] = lax.dot_general(
                hot, r, (((0,), (0,)), ((), ())), preferred_element_type=F32
            ).astype(BF16)

            @pl.when(head)
            def _():
                chain_copy(zp, c).start()

            return 0

        lax.fori_loop(0, CHUNKS, col, 0)

    def place(d, side):
        zp = z + d * (1 - 2 * side)
        ok = (zp >= 0) & (zp < zs) & ((d > 0) | (side == 0))
        return zp, ok

    def sides(d, fn):
        def one(side, _):
            zp, ok = place(d, side)

            @pl.when(ok)
            def _():
                fn(zp)

            return 0

        lax.fori_loop(0, 2, one, 0)

    for c in owns:
        c.wait()
    for c in loads:
        c.wait()

    def step(d, _):
        for k in range(2):
            sides(d, lambda zp: take(k, zp, d))
        sides(d, work)
        sides(d, combine)
        return 0

    lax.fori_loop(0, zs, step, 0)

    def relay(up, zp):
        def col(c, _):
            chain_wait(up, zp, c)
            part[zp, c] = (part[zp, c].astype(F32) + chain[up, zp, c].astype(F32)).astype(BF16)
            chain_copy(zp, c).start()
            return 0

        lax.fori_loop(0, CHUNKS, col, 0)

    def hop(k, _):
        down = zs - 1 - k

        @pl.when((z > 0) & (z < k))
        def _():
            relay(1, k)

        @pl.when((z < zs - 1) & (z > down))
        def _():
            relay(0, down)

        return 0

    lax.fori_loop(1, zs, hop, 0)

    def pipe_copy(c):
        at = pl.ds(c * cols, cols)
        return remote(
            stage.at[c], out_ref.at[:, at], p_send.at[c], p_recv.at[c], pipe=prev_pipe
        )

    for c in range(CHUNKS):
        stage[c] = part[z, c]
        has_below, has_above = z > 0, z < zs - 1

        @pl.when(has_below & has_above)
        def _():
            chain_wait(1, z, c)
            chain_wait(0, z, c)
            stage[c] = (
                part[z, c].astype(F32) + chain[1, z, c].astype(F32) + chain[0, z, c].astype(F32)
            ).astype(BF16)

        @pl.when(has_below & (z == zs - 1))
        def _():
            chain_wait(1, z, c)
            stage[c] = (part[z, c].astype(F32) + chain[1, z, c].astype(F32)).astype(BF16)

        @pl.when(has_above & (z == 0))
        def _():
            chain_wait(0, z, c)
            stage[c] = (part[z, c].astype(F32) + chain[0, z, c].astype(F32)).astype(BF16)

        @pl.when(pipe > 0)
        def _():
            pipe_copy(c).start()

    for i in range(1, n):
        gg_wait(lax.rem(me + i, n))
    ggbuf[me] = ggout[me]
    total = ggbuf[0]
    for e in range(1, n):
        total = total + ggbuf[e]
    gg_ref[...] = total.astype(BF16)

    for k in range(2):
        @pl.when(z < zs - 1)
        def _():
            own_copy(k, 1).wait_send()

        @pl.when(z > 0)
        def _():
            own_copy(k, 0).wait_send()

    def drain(zp, _):
        @pl.when(can_fwd(zp))
        def _():
            for k in range(2):
                fwd_copy(k, zp).wait_send()

        for i in range(1, xs):
            for k in range(2):
                xsel_copy(k, zp, i).wait_send()

            def xcol(c, _):
                xret_copy(zp, c, i).wait_send()
                return 0

            lax.fori_loop(0, CHUNKS, xcol, 0)

        @pl.when(zp != z)
        def _():
            def ccol(c, _):
                chain_copy(zp, c).wait_send()
                return 0

            lax.fori_loop(0, CHUNKS, ccol, 0)

        return 0

    lax.fori_loop(0, zs, drain, 0)
    for i in range(1, n):
        meta_copy(i).wait_send()
        gg_copy(lax.rem(me + i, n)).wait_send()

    @pl.when(pipe > 0)
    def _():
        for c in range(CHUNKS):
            pipe_copy(c).wait_send()

    @pl.when(pipe < pipes - 1)
    def _():
        for c in range(CHUNKS):
            pipe_copy(c).wait_recv()

    @pl.when(pipe == pipes - 1)
    def _():
        out_ref[...] = jnp.zeros(out_ref.shape, BF16)


def local(pipes, tokens, out_grad, gates, expert_ids, w_gate, w_up, w_down):
    rows, width = tokens.shape[1:]
    top = expert_ids.shape[2]
    n = lax.axis_size("expert")
    xs = 1 << ((n.bit_length() - 1) // 2)
    zs = n // xs
    cap = max(2, 2 * rows * top // n)
    hidden = w_gate.shape[3]
    slots = xs * cap
    cols = width // CHUNKS
    dma = pltpu.SemaphoreType.DMA
    vmem = pl.BlockSpec(memory_space=pltpu.VMEM)
    hbm = pl.BlockSpec(memory_space=pl.ANY)
    arrived, gg = pl.pallas_call(
        functools.partial(kernel, pipes, zs, xs, cap),
        out_shape=(
            jax.ShapeDtypeStruct((rows, width), BF16),
            jax.ShapeDtypeStruct((top, rows), BF16),
        ),
        in_specs=[hbm, hbm, vmem, vmem, hbm, hbm, hbm],
        out_specs=(vmem, vmem),
        scratch_shapes=[
            pltpu.VMEM((width, hidden), BF16),
            pltpu.VMEM((width, hidden), BF16),
            pltpu.VMEM((hidden, width), BF16),
            pltpu.VMEM((2, zs, rows, width), BF16),
            pltpu.VMEM((2, zs, xs, cap, width), BF16),
            pltpu.VMEM((2, zs, xs, cap, width), BF16),
            pltpu.VMEM((8, 128), F32),
            pltpu.VMEM((8, 128), F32),
            pltpu.VMEM((8, 128), F32),
            pltpu.VMEM((slots, hidden), BF16),
            pltpu.VMEM((slots, hidden), BF16),
            pltpu.VMEM((slots, 1), F32),
            pltpu.VMEM((zs, CHUNKS, xs, cap, cols), BF16),
            pltpu.VMEM((zs, CHUNKS, xs, cap, cols), BF16),
            pltpu.VMEM((zs, CHUNKS, rows, cols), BF16),
            pltpu.VMEM((2, zs, CHUNKS, rows, cols), BF16),
            pltpu.VMEM((CHUNKS, rows, cols), BF16),
            pltpu.VMEM((n, 8, rows), F32),
            pltpu.VMEM((n, top, rows), F32),
            pltpu.VMEM((n, top, rows), F32),
            dma((3,)),
            dma((2,)),
            dma((2, 2)),
            dma((2, zs)),
            dma((2, zs)),
            dma((2, zs, xs)),
            dma((2, zs, xs)),
            dma((n,)),
            dma((n,)),
            dma((n,)),
            dma((n,)),
            dma((zs, CHUNKS, xs)),
            dma((zs, CHUNKS, xs)),
            dma((zs, CHUNKS)),
            dma((2, zs, CHUNKS)),
            dma((CHUNKS,)),
            dma((CHUNKS,)),
        ],
        compiler_params=pltpu.CompilerParams(
            collective_id=0, has_side_effects=True, vmem_limit_bytes=56 * 1024 * 1024
        ),
    )(
        tokens[0], out_grad[0], expert_ids[0].T, gates[0].T,
        w_gate[0, 0], w_up[0, 0], w_down[0, 0],
    )
    return arrived[None], gg.T[None]


def solution(mesh):
    row = P("pipe", "expert", None)
    weight = P("pipe", "expert", None, None)
    return jax.shard_map(
        functools.partial(local, mesh.shape["pipe"]),
        mesh=mesh,
        in_specs=(row, row, row, row, weight, weight, weight),
        out_specs=(row, row),
        check_vma=False,
    )
```

```python
import functools
import jax
import jax.numpy as jnp
from jax import lax
from jax.experimental import pallas as pl
from jax.experimental.pallas import tpu as pltpu
from jax.sharding import PartitionSpec as P

F32 = jnp.float32
BF16 = jnp.bfloat16
CHUNKS = 4
PIECES = 2


def kernel(
    pipes, zs, xs, cap,
    tok_ref, grad_ref, ids_ref, gates_ref, wg_ref, wu_ref, wd_ref,
    out_ref, gg_ref,
    wg, wu, wd, blk, sel_out, sel_in, gate_s, up_s, dgate_s, dup_s, slot_gate,
    ret_out, ret_in, part, chain, stage, meta, ggbuf, ggout,
    w_sem, own_sem, own_send, fwd_send, blk_recv, xs_send, xs_recv, m_send, m_recv,
    g_send, g_recv, xr_send, xr_recv, ch_send, ch_recv, p_send, p_recv,
):
    n = zs * xs
    pipe = lax.axis_index("pipe")
    me = lax.axis_index("expert")
    z, x = me // xs, me % xs
    rows, width = tok_ref.shape
    cols = width // CHUNKS
    slots = xs * cap
    hidden = wg.shape[1]
    span = width // PIECES
    htile = 256
    mesh_ids = pl.DeviceIdType.MESH

    def remote(src, dst, ssem, rsem, **dev):
        return pltpu.make_async_remote_copy(
            src_ref=src, dst_ref=dst, send_sem=ssem, recv_sem=rsem,
            device_id=dev, device_id_type=mesh_ids,
        )

    loads = [
        pltpu.make_async_copy(wg_ref, wg, w_sem.at[0]),
        pltpu.make_async_copy(wu_ref, wu, w_sem.at[1]),
        pltpu.make_async_copy(wd_ref, wd, w_sem.at[2]),
    ]
    owns = [
        pltpu.make_async_copy(
            (tok_ref, grad_ref)[k].at[:, pl.ds(p * span, span)], blk.at[k, p, z], own_sem.at[k, p]
        )
        for k in range(2)
        for p in range(PIECES)
    ]
    for c in owns + loads:
        c.start()

    barrier = pltpu.get_barrier_semaphore()
    prev_pipe = lax.rem(pipe + pipes - 1, pipes)
    next_pipe = lax.rem(pipe + 1, pipes)
    for i in range(1, n):
        pl.semaphore_signal(
            barrier, inc=1, device_id={"expert": lax.rem(me + i, n)}, device_id_type=mesh_ids
        )
    for other in (prev_pipe, next_pipe):
        pl.semaphore_signal(barrier, inc=1, device_id={"pipe": other}, device_id_type=mesh_ids)
    pl.semaphore_wait(barrier, n + 1)

    def own_copy(k, p, up):
        src = (tok_ref, grad_ref)[k].at[:, pl.ds(p * span, span)]
        return remote(
            src, blk.at[k, p, z], own_send.at[up, k, p], blk_recv.at[k, p, z],
            expert=me + xs if up else me - xs,
        )

    pieces = [(k, p) for k in range(2) for p in range(PIECES)]
    for k, p in pieces:
        @pl.when(z < zs - 1)
        def _():
            own_copy(k, p, 1).start()

        @pl.when(z > 0)
        def _():
            own_copy(k, p, 0).start()

    ids = ids_ref[...]
    sub = lax.broadcasted_iota(jnp.int32, (n, rows), 0)
    hot0 = (sub == ids[0:1]).astype(F32)
    hot1 = (sub == ids[1:2]).astype(F32)
    before = (
        lax.broadcasted_iota(jnp.int32, (rows, rows), 0)
        < lax.broadcasted_iota(jnp.int32, (rows, rows), 1)
    ).astype(F32).astype(BF16)
    earlier = jnp.dot((hot0 + hot1).astype(BF16), before, preferred_element_type=F32)
    idf = ids.astype(F32) * cap
    pos0 = idf[0:1] + jnp.sum(hot0 * earlier, axis=0, keepdims=True)
    pos1 = idf[1:2] + jnp.sum(hot1 * earlier, axis=0, keepdims=True)
    meta[me, 0:1] = pos0
    meta[me, 1:2] = pos1
    meta[me, 2:4] = gates_ref[...]
    meta[me, 4:8] = jnp.zeros((4, rows), F32)

    def meta_copy(i):
        return remote(
            meta.at[me], meta.at[me], m_send.at[i], m_recv.at[me], expert=lax.rem(me + i, n)
        )

    def meta_wait(i):
        e = lax.rem(me + i, n)
        remote(meta.at[e], meta.at[e], m_send.at[i], m_recv.at[e], expert=e).wait_recv()

    for i in range(1, n):
        meta_copy(i).start()

    def onehot(e, first, count):
        want = (first + lax.broadcasted_iota(jnp.int32, (count, rows), 0)).astype(F32)
        m = meta[e]
        return (want == m[0:1]).astype(F32), (want == m[1:2]).astype(F32), m

    def fwd_copy(k, p, zp):
        return remote(
            blk.at[k, p, zp], blk.at[k, p, zp], fwd_send.at[k, p, zp], blk_recv.at[k, p, zp],
            expert=jnp.where(zp > z, me - xs, me + xs),
        )

    def can_fwd(zp):
        return ((zp > z) & (z > 0)) | ((zp < z) & (z < zs - 1))

    def xsel_copy(k, p, zp, i):
        to = lax.rem(x + i, xs)
        return remote(
            sel_out.at[k, p, zp, to], sel_in.at[k, p, zp, x], xs_send.at[k, p, zp, i],
            xs_recv.at[k, p, zp, x], expert=z * xs + to,
        )

    def xsel_wait(k, p, zp, i):
        fr = lax.rem(x + i, xs)
        remote(
            sel_out.at[k, p, zp, fr], sel_in.at[k, p, zp, fr], xs_send.at[k, p, zp, i],
            xs_recv.at[k, p, zp, fr], expert=z * xs + fr,
        ).wait_recv()

    def xret_copy(zp, c, i):
        to = lax.rem(x + i, xs)
        return remote(
            ret_out.at[zp, c, to], ret_in.at[zp, c, x], xr_send.at[zp, c, i],
            xr_recv.at[zp, c, x], expert=z * xs + to,
        )

    def xret_wait(zp, c, i):
        fr = lax.rem(x + i, xs)
        remote(
            ret_out.at[zp, c, fr], ret_in.at[zp, c, fr], xr_send.at[zp, c, i],
            xr_recv.at[zp, c, fr], expert=z * xs + fr,
        ).wait_recv()

    def chain_copy(zp, c):
        up = (zp > z).astype(jnp.int32)
        return remote(
            part.at[zp, c], chain.at[up, zp, c], ch_send.at[zp, c], ch_recv.at[up, zp, c],
            expert=jnp.where(zp > z, me + xs, me - xs),
        )

    def chain_wait(up, zp, c):
        remote(
            part.at[zp, c], chain.at[up, zp, c], ch_send.at[zp, c], ch_recv.at[up, zp, c],
            expert=jnp.where(up == 1, me - xs, me + xs),
        ).wait_recv()

    def gg_copy(e):
        return remote(ggout.at[e], ggbuf.at[me], g_send.at[e], g_recv.at[me], expert=e)

    def gg_wait(e):
        remote(ggout.at[e], ggbuf.at[e], g_send.at[e], g_recv.at[e], expert=e).wait_recv()

    def take(k, zp, d):
        o0, o1, _ = onehot(zp * xs + x, z * slots, slots)
        hot = (o0 + o1).astype(BF16)

        def piece(p, _):
            @pl.when(d > 0)
            def _():
                fwd_copy(k, p, zp).wait_recv()

                @pl.when(can_fwd(zp))
                def _():
                    fwd_copy(k, p, zp).start()

            got = jnp.dot(hot, blk[k, p, zp], preferred_element_type=F32).astype(BF16)
            sel_out[k, p, zp] = got.reshape(xs, cap, span)
            for i in range(1, xs):
                xsel_copy(k, p, zp, i).start()
            sel_in[k, p, zp, x] = sel_out[k, p, zp, x]
            return 0

        lax.fori_loop(0, PIECES, piece, 0)

    def xsel_arrived(k, zp):
        for p in range(PIECES):
            for i in range(1, xs):
                xsel_wait(k, p, zp, i)

    def work(zp):
        contract_last = (((1,), (1,)), ((), ()))
        xsel_arrived(0, zp)

        def tile_up(h, _):
            at = pl.ds(pl.multiple_of(h * htile, htile), htile)
            gate = jnp.zeros((slots, htile), F32)
            up = jnp.zeros((slots, htile), F32)
            for p in range(PIECES):
                a = sel_in[0, p, zp].reshape(slots, span)
                depth = slice(p * span, (p + 1) * span)
                gate = gate + jnp.dot(a, wg[depth, at], preferred_element_type=F32)
                up = up + jnp.dot(a, wu[depth, at], preferred_element_type=F32)
            gate_s[:, at] = gate
            up_s[:, at] = up
            return 0

        lax.fori_loop(0, hidden // htile, tile_up, 0)
        xsel_arrived(1, zp)

        def tile(h, _):
            at = pl.ds(pl.multiple_of(h * htile, htile), htile)
            dh = jnp.zeros((slots, htile), F32)
            for p in range(PIECES):
                b = sel_in[1, p, zp].reshape(slots, span)
                depth = slice(p * span, (p + 1) * span)
                dh = dh + lax.dot_general(
                    b, wd[at, depth], contract_last, preferred_element_type=F32
                )
            gate = gate_s[:, at]
            up = up_s[:, at]
            sig = jax.nn.sigmoid(gate)
            act = gate * sig
            dup_s[:, at] = (dh * act).astype(BF16)
            dgate_s[:, at] = (dh * up * sig * (1.0 + gate * (1.0 - sig))).astype(BF16)
            return _ + jnp.sum(dh * (act * up), axis=-1, keepdims=True)

        gg = lax.fori_loop(0, hidden // htile, tile, jnp.zeros((slots, 1), F32))
        for s in range(xs):
            e = zp * xs + s
            o0, o1, m = onehot(e, me * cap, cap)
            slot_gate[s * cap:(s + 1) * cap] = jnp.sum(
                o0 * m[2:3] + o1 * m[3:4], axis=1, keepdims=True
            )
            mine = gg[s * cap:(s + 1) * cap]
            ggout[e, 0:1] = jnp.sum(o0 * mine, axis=0, keepdims=True)
            ggout[e, 1:2] = jnp.sum(o1 * mine, axis=0, keepdims=True)

            @pl.when(e != me)
            def _():
                gg_copy(e).start()

        def col(c, _):
            at = pl.ds(pl.multiple_of(c * cols, cols), cols)
            r = lax.dot_general(dgate_s[...], wg[at, :], contract_last, preferred_element_type=F32)
            r = r + lax.dot_general(dup_s[...], wu[at, :], contract_last, preferred_element_type=F32)
            r = (r * slot_gate[...]).astype(BF16)
            ret_out[zp, c] = r.reshape(xs, cap, cols)
            for i in range(1, xs):
                xret_copy(zp, c, i).start()
            ret_in[zp, c, x] = ret_out[zp, c, x]
            return 0

        lax.fori_loop(0, CHUNKS, col, 0)

    def combine(zp):
        o0, o1, _ = onehot(zp * xs + x, z * slots, slots)
        hot = (o0 + o1).astype(BF16)
        head = ((z == 0) & (zp > 0)) | ((z == zs - 1) & (zp < z))

        def col(c, _):
            for i in range(1, xs):
                xret_wait(zp, c, i)
            r = ret_in[zp, c].reshape(slots, cols)
            part[zp, c] = lax.dot_general(
                hot, r, (((0,), (0,)), ((), ())), preferred_element_type=F32
            ).astype(BF16)

            @pl.when(head)
            def _():
                chain_copy(zp, c).start()

            return 0

        lax.fori_loop(0, CHUNKS, col, 0)

    def place(d, side):
        zp = z + d * (1 - 2 * side)
        ok = (zp >= 0) & (zp < zs) & ((d > 0) | ((d == 0) & (side == 0)))
        return zp, ok

    def sides(d, fn):
        def one(side, _):
            zp, ok = place(d, side)

            @pl.when(ok)
            def _():
                fn(zp)

            return 0

        lax.fori_loop(0, 2, one, 0)

    for c in owns:
        c.wait()

    def step(u, _):
        d, k = u // 2, u % 2
        sides(d, lambda zp: take(k, zp, d))

        @pl.when(u == 1)
        def _():
            for c in loads:
                c.wait()
            for i in range(1, n):
                meta_wait(i)

        sides(jnp.where(u == 1, 0, jnp.where((k == 0) & (d >= 2), d - 1, -1)), work)
        sides(jnp.where(k == 1, d - 1, -1), combine)
        return 0

    lax.fori_loop(0, 2 * zs + 2, step, 0)

    def relay(up, zp):
        def col(c, _):
            chain_wait(up, zp, c)
            part[zp, c] = (part[zp, c].astype(F32) + chain[up, zp, c].astype(F32)).astype(BF16)
            chain_copy(zp, c).start()
            return 0

        lax.fori_loop(0, CHUNKS, col, 0)

    def hop(k, _):
        down = zs - 1 - k

        @pl.when((z > 0) & (z < k))
        def _():
            relay(1, k)

        @pl.when((z < zs - 1) & (z > down))
        def _():
            relay(0, down)

        return 0

    lax.fori_loop(1, zs, hop, 0)

    def pipe_copy(c):
        at = pl.ds(c * cols, cols)
        return remote(
            stage.at[c], out_ref.at[:, at], p_send.at[c], p_recv.at[c], pipe=prev_pipe
        )

    for c in range(CHUNKS):
        stage[c] = part[z, c]
        has_below, has_above = z > 0, z < zs - 1

        @pl.when(has_below & has_above)
        def _():
            chain_wait(1, z, c)
            chain_wait(0, z, c)
            stage[c] = (
                part[z, c].astype(F32) + chain[1, z, c].astype(F32) + chain[0, z, c].astype(F32)
            ).astype(BF16)

        @pl.when(has_below & (z == zs - 1))
        def _():
            chain_wait(1, z, c)
            stage[c] = (part[z, c].astype(F32) + chain[1, z, c].astype(F32)).astype(BF16)

        @pl.when(has_above & (z == 0))
        def _():
            chain_wait(0, z, c)
            stage[c] = (part[z, c].astype(F32) + chain[0, z, c].astype(F32)).astype(BF16)

        @pl.when(pipe > 0)
        def _():
            pipe_copy(c).start()

    for i in range(1, n):
        gg_wait(lax.rem(me + i, n))
    ggbuf[me] = ggout[me]
    total = ggbuf[0]
    for e in range(1, n):
        total = total + ggbuf[e]
    gg_ref[...] = total.astype(BF16)

    for k, p in pieces:
        @pl.when(z < zs - 1)
        def _():
            own_copy(k, p, 1).wait_send()

        @pl.when(z > 0)
        def _():
            own_copy(k, p, 0).wait_send()

    def drain(zp, _):
        @pl.when(can_fwd(zp))
        def _():
            for k, p in pieces:
                fwd_copy(k, p, zp).wait_send()

        for i in range(1, xs):
            for k, p in pieces:
                xsel_copy(k, p, zp, i).wait_send()

            def xcol(c, _):
                xret_copy(zp, c, i).wait_send()
                return 0

            lax.fori_loop(0, CHUNKS, xcol, 0)

        @pl.when(zp != z)
        def _():
            def ccol(c, _):
                chain_copy(zp, c).wait_send()
                return 0

            lax.fori_loop(0, CHUNKS, ccol, 0)

        return 0

    lax.fori_loop(0, zs, drain, 0)
    for i in range(1, n):
        meta_copy(i).wait_send()
        gg_copy(lax.rem(me + i, n)).wait_send()

    @pl.when(pipe > 0)
    def _():
        for c in range(CHUNKS):
            pipe_copy(c).wait_send()

    @pl.when(pipe < pipes - 1)
    def _():
        for c in range(CHUNKS):
            pipe_copy(c).wait_recv()

    @pl.when(pipe == pipes - 1)
    def _():
        out_ref[...] = jnp.zeros(out_ref.shape, BF16)


def local(pipes, tokens, out_grad, gates, expert_ids, w_gate, w_up, w_down):
    rows, width = tokens.shape[1:]
    top = expert_ids.shape[2]
    n = lax.axis_size("expert")
    xs = 1 << ((n.bit_length() - 1) // 2)
    zs = n // xs
    cap = max(2, 2 * rows * top // n)
    hidden = w_gate.shape[3]
    slots = xs * cap
    cols = width // CHUNKS
    span = width // PIECES
    dma = pltpu.SemaphoreType.DMA
    vmem = pl.BlockSpec(memory_space=pltpu.VMEM)
    hbm = pl.BlockSpec(memory_space=pl.ANY)
    arrived, gg = pl.pallas_call(
        functools.partial(kernel, pipes, zs, xs, cap),
        out_shape=(
            jax.ShapeDtypeStruct((rows, width), BF16),
            jax.ShapeDtypeStruct((top, rows), BF16),
        ),
        in_specs=[hbm, hbm, vmem, vmem, hbm, hbm, hbm],
        out_specs=(vmem, vmem),
        scratch_shapes=[
            pltpu.VMEM((width, hidden), BF16),
            pltpu.VMEM((width, hidden), BF16),
            pltpu.VMEM((hidden, width), BF16),
            pltpu.VMEM((2, PIECES, zs, rows, span), BF16),
            pltpu.VMEM((2, PIECES, zs, xs, cap, span), BF16),
            pltpu.VMEM((2, PIECES, zs, xs, cap, span), BF16),
            pltpu.VMEM((slots, hidden), F32),
            pltpu.VMEM((slots, hidden), F32),
            pltpu.VMEM((slots, hidden), BF16),
            pltpu.VMEM((slots, hidden), BF16),
            pltpu.VMEM((slots, 1), F32),
            pltpu.VMEM((zs, CHUNKS, xs, cap, cols), BF16),
            pltpu.VMEM((zs, CHUNKS, xs, cap, cols), BF16),
            pltpu.VMEM((zs, CHUNKS, rows, cols), BF16),
            pltpu.VMEM((2, zs, CHUNKS, rows, cols), BF16),
            pltpu.VMEM((CHUNKS, rows, cols), BF16),
            pltpu.VMEM((n, 8, rows), F32),
            pltpu.VMEM((n, top, rows), F32),
            pltpu.VMEM((n, top, rows), F32),
            dma((3,)),
            dma((2, PIECES)),
            dma((2, 2, PIECES)),
            dma((2, PIECES, zs)),
            dma((2, PIECES, zs)),
            dma((2, PIECES, zs, xs)),
            dma((2, PIECES, zs, xs)),
            dma((n,)),
            dma((n,)),
            dma((n,)),
            dma((n,)),
            dma((zs, CHUNKS, xs)),
            dma((zs, CHUNKS, xs)),
            dma((zs, CHUNKS)),
            dma((2, zs, CHUNKS)),
            dma((CHUNKS,)),
            dma((CHUNKS,)),
        ],
        compiler_params=pltpu.CompilerParams(
            collective_id=0, has_side_effects=True, vmem_limit_bytes=56 * 1024 * 1024
        ),
    )(
        tokens[0], out_grad[0], expert_ids[0].T, gates[0].T,
        w_gate[0, 0], w_up[0, 0], w_down[0, 0],
    )
    return arrived[None], gg.T[None]


def solution(mesh):
    row = P("pipe", "expert", None)
    weight = P("pipe", "expert", None, None)
    return jax.shard_map(
        functools.partial(local, mesh.shape["pipe"]),
        mesh=mesh,
        in_specs=(row, row, row, row, weight, weight, weight),
        out_specs=(row, row),
        check_vma=False,
    )
```

```python
import functools
import jax
import jax.numpy as jnp
from jax import lax
from jax.experimental import pallas as pl
from jax.experimental.pallas import tpu as pltpu
from jax.sharding import PartitionSpec as P

F32 = jnp.float32
BF16 = jnp.bfloat16
CHUNKS = 2
PIECES = 1


def kernel(
    pipes, zs, xs, cap,
    tok_ref, grad_ref, ids_ref, gates_ref, wg_ref, wu_ref, wd_ref,
    out_ref, gg_ref,
    wg, wu, wd, blk, sel_out, sel_in, gate_s, up_s, dgate_s, dup_s, slot_gate,
    ret_out, ret_in, part, chain, stage, meta, ggbuf, ggout,
    w_sem, own_sem, own_send, fwd_send, blk_recv, xs_send, xs_recv, m_send, m_recv,
    g_send, g_recv, xr_send, xr_recv, ch_send, ch_recv, p_send, p_recv,
):
    n = zs * xs
    pipe = lax.axis_index("pipe")
    me = lax.axis_index("expert")
    z, x = me // xs, me % xs
    rows, width = tok_ref.shape
    cols = width // CHUNKS
    slots = xs * cap
    hidden = wg.shape[1]
    span = width // PIECES
    htile = 256
    mesh_ids = pl.DeviceIdType.MESH

    def remote(src, dst, ssem, rsem, **dev):
        return pltpu.make_async_remote_copy(
            src_ref=src, dst_ref=dst, send_sem=ssem, recv_sem=rsem,
            device_id=dev, device_id_type=mesh_ids,
        )

    loads = [
        pltpu.make_async_copy(wg_ref, wg, w_sem.at[0]),
        pltpu.make_async_copy(wu_ref, wu, w_sem.at[1]),
        pltpu.make_async_copy(wd_ref, wd, w_sem.at[2]),
    ]
    owns = [
        pltpu.make_async_copy(
            (tok_ref, grad_ref)[k].at[:, pl.ds(p * span, span)], blk.at[k, p, z], own_sem.at[k, p]
        )
        for k in range(2)
        for p in range(PIECES)
    ]
    for c in owns + loads:
        c.start()

    barrier = pltpu.get_barrier_semaphore()
    prev_pipe = lax.rem(pipe + pipes - 1, pipes)
    next_pipe = lax.rem(pipe + 1, pipes)
    for i in range(1, n):
        pl.semaphore_signal(
            barrier, inc=1, device_id={"expert": lax.rem(me + i, n)}, device_id_type=mesh_ids
        )
    for other in (prev_pipe, next_pipe):
        pl.semaphore_signal(barrier, inc=1, device_id={"pipe": other}, device_id_type=mesh_ids)
    pl.semaphore_wait(barrier, n + 1)

    def own_copy(k, p, up):
        src = (tok_ref, grad_ref)[k].at[:, pl.ds(p * span, span)]
        return remote(
            src, blk.at[k, p, z], own_send.at[up, k, p], blk_recv.at[k, p, z],
            expert=me + xs if up else me - xs,
        )

    pieces = [(k, p) for k in range(2) for p in range(PIECES)]
    for k, p in pieces:
        @pl.when(z < zs - 1)
        def _():
            own_copy(k, p, 1).start()

        @pl.when(z > 0)
        def _():
            own_copy(k, p, 0).start()

    ids = ids_ref[...]
    sub = lax.broadcasted_iota(jnp.int32, (n, rows), 0)
    hot0 = (sub == ids[0:1]).astype(F32)
    hot1 = (sub == ids[1:2]).astype(F32)
    before = (
        lax.broadcasted_iota(jnp.int32, (rows, rows), 0)
        < lax.broadcasted_iota(jnp.int32, (rows, rows), 1)
    ).astype(F32).astype(BF16)
    earlier = jnp.dot((hot0 + hot1).astype(BF16), before, preferred_element_type=F32)
    idf = ids.astype(F32) * cap
    pos0 = idf[0:1] + jnp.sum(hot0 * earlier, axis=0, keepdims=True)
    pos1 = idf[1:2] + jnp.sum(hot1 * earlier, axis=0, keepdims=True)
    meta[me, 0:1] = pos0
    meta[me, 1:2] = pos1
    meta[me, 2:4] = gates_ref[...]
    meta[me, 4:8] = jnp.zeros((4, rows), F32)

    def meta_copy(i):
        return remote(
            meta.at[me], meta.at[me], m_send.at[i], m_recv.at[me], expert=lax.rem(me + i, n)
        )

    def meta_wait(i):
        e = lax.rem(me + i, n)
        remote(meta.at[e], meta.at[e], m_send.at[i], m_recv.at[e], expert=e).wait_recv()

    for i in range(1, n):
        meta_copy(i).start()

    def onehot(e, first, count):
        want = (first + lax.broadcasted_iota(jnp.int32, (count, rows), 0)).astype(F32)
        m = meta[e]
        return (want == m[0:1]).astype(F32), (want == m[1:2]).astype(F32), m

    def fwd_copy(k, p, zp):
        return remote(
            blk.at[k, p, zp], blk.at[k, p, zp], fwd_send.at[k, p, zp], blk_recv.at[k, p, zp],
            expert=jnp.where(zp > z, me - xs, me + xs),
        )

    def can_fwd(zp):
        return ((zp > z) & (z > 0)) | ((zp < z) & (z < zs - 1))

    def xsel_copy(k, p, zp, i):
        to = lax.rem(x + i, xs)
        return remote(
            sel_out.at[k, p, zp, to], sel_in.at[k, p, zp, x], xs_send.at[k, p, zp, i],
            xs_recv.at[k, p, zp, x], expert=z * xs + to,
        )

    def xsel_wait(k, p, zp, i):
        fr = lax.rem(x + i, xs)
        remote(
            sel_out.at[k, p, zp, fr], sel_in.at[k, p, zp, fr], xs_send.at[k, p, zp, i],
            xs_recv.at[k, p, zp, fr], expert=z * xs + fr,
        ).wait_recv()

    def xret_copy(zp, c, i):
        to = lax.rem(x + i, xs)
        return remote(
            ret_out.at[zp, c, to], ret_in.at[zp, c, x], xr_send.at[zp, c, i],
            xr_recv.at[zp, c, x], expert=z * xs + to,
        )

    def xret_wait(zp, c, i):
        fr = lax.rem(x + i, xs)
        remote(
            ret_out.at[zp, c, fr], ret_in.at[zp, c, fr], xr_send.at[zp, c, i],
            xr_recv.at[zp, c, fr], expert=z * xs + fr,
        ).wait_recv()

    def chain_copy(zp, c):
        up = (zp > z).astype(jnp.int32)
        return remote(
            part.at[zp, c], chain.at[up, zp, c], ch_send.at[zp, c], ch_recv.at[up, zp, c],
            expert=jnp.where(zp > z, me + xs, me - xs),
        )

    def chain_wait(up, zp, c):
        remote(
            part.at[zp, c], chain.at[up, zp, c], ch_send.at[zp, c], ch_recv.at[up, zp, c],
            expert=jnp.where(up == 1, me - xs, me + xs),
        ).wait_recv()

    def gg_copy(e):
        return remote(ggout.at[e], ggbuf.at[me], g_send.at[e], g_recv.at[me], expert=e)

    def gg_wait(e):
        remote(ggout.at[e], ggbuf.at[e], g_send.at[e], g_recv.at[e], expert=e).wait_recv()

    def take(k, zp, d):
        o0, o1, _ = onehot(zp * xs + x, z * slots, slots)
        hot = (o0 + o1).astype(BF16)

        def piece(p, _):
            @pl.when(d > 0)
            def _():
                fwd_copy(k, p, zp).wait_recv()

                @pl.when(can_fwd(zp))
                def _():
                    fwd_copy(k, p, zp).start()

            got = jnp.dot(hot, blk[k, p, zp], preferred_element_type=F32).astype(BF16)
            sel_out[k, p, zp] = got.reshape(xs, cap, span)
            for i in range(1, xs):
                xsel_copy(k, p, zp, i).start()
            sel_in[k, p, zp, x] = sel_out[k, p, zp, x]
            return 0

        lax.fori_loop(0, PIECES, piece, 0)

    def xsel_arrived(k, zp):
        for p in range(PIECES):
            for i in range(1, xs):
                xsel_wait(k, p, zp, i)

    def work(zp):
        contract_last = (((1,), (1,)), ((), ()))
        xsel_arrived(0, zp)

        def tile_up(h, _):
            at = pl.ds(pl.multiple_of(h * htile, htile), htile)
            gate = jnp.zeros((slots, htile), F32)
            up = jnp.zeros((slots, htile), F32)
            for p in range(PIECES):
                a = sel_in[0, p, zp].reshape(slots, span)
                depth = slice(p * span, (p + 1) * span)
                gate = gate + jnp.dot(a, wg[depth, at], preferred_element_type=F32)
                up = up + jnp.dot(a, wu[depth, at], preferred_element_type=F32)
            gate_s[:, at] = gate
            up_s[:, at] = up
            return 0

        lax.fori_loop(0, hidden // htile, tile_up, 0)
        xsel_arrived(1, zp)

        def tile(h, _):
            at = pl.ds(pl.multiple_of(h * htile, htile), htile)
            dh = jnp.zeros((slots, htile), F32)
            for p in range(PIECES):
                b = sel_in[1, p, zp].reshape(slots, span)
                depth = slice(p * span, (p + 1) * span)
                dh = dh + lax.dot_general(
                    b, wd[at, depth], contract_last, preferred_element_type=F32
                )
            gate = gate_s[:, at]
            up = up_s[:, at]
            sig = jax.nn.sigmoid(gate)
            act = gate * sig
            dup_s[:, at] = (dh * act).astype(BF16)
            dgate_s[:, at] = (dh * up * sig * (1.0 + gate * (1.0 - sig))).astype(BF16)
            return _ + jnp.sum(dh * (act * up), axis=-1, keepdims=True)

        gg = lax.fori_loop(0, hidden // htile, tile, jnp.zeros((slots, 1), F32))
        for s in range(xs):
            e = zp * xs + s
            o0, o1, m = onehot(e, me * cap, cap)
            slot_gate[s * cap:(s + 1) * cap] = jnp.sum(
                o0 * m[2:3] + o1 * m[3:4], axis=1, keepdims=True
            )
            mine = gg[s * cap:(s + 1) * cap]
            ggout[e, 0:1] = jnp.sum(o0 * mine, axis=0, keepdims=True)
            ggout[e, 1:2] = jnp.sum(o1 * mine, axis=0, keepdims=True)

            @pl.when(e != me)
            def _():
                gg_copy(e).start()

        def col(c, _):
            at = pl.ds(pl.multiple_of(c * cols, cols), cols)
            r = lax.dot_general(dgate_s[...], wg[at, :], contract_last, preferred_element_type=F32)
            r = r + lax.dot_general(dup_s[...], wu[at, :], contract_last, preferred_element_type=F32)
            r = (r * slot_gate[...]).astype(BF16)
            ret_out[zp, c] = r.reshape(xs, cap, cols)
            for i in range(1, xs):
                xret_copy(zp, c, i).start()
            ret_in[zp, c, x] = ret_out[zp, c, x]
            return 0

        lax.fori_loop(0, CHUNKS, col, 0)

    def combine(zp):
        o0, o1, _ = onehot(zp * xs + x, z * slots, slots)
        hot = (o0 + o1).astype(BF16)
        head = ((z == 0) & (zp > 0)) | ((z == zs - 1) & (zp < z))

        def col(c, _):
            for i in range(1, xs):
                xret_wait(zp, c, i)
            r = ret_in[zp, c].reshape(slots, cols)
            part[zp, c] = lax.dot_general(
                hot, r, (((0,), (0,)), ((), ())), preferred_element_type=F32
            ).astype(BF16)

            @pl.when(head)
            def _():
                chain_copy(zp, c).start()

            return 0

        lax.fori_loop(0, CHUNKS, col, 0)

    def place(d, side):
        zp = z + d * (1 - 2 * side)
        ok = (zp >= 0) & (zp < zs) & ((d > 0) | ((d == 0) & (side == 0)))
        return zp, ok

    def sides(d, fn):
        def one(side, _):
            zp, ok = place(d, side)

            @pl.when(ok)
            def _():
                fn(zp)

            return 0

        lax.fori_loop(0, 2, one, 0)

    for c in owns:
        c.wait()

    def step(u, _):
        d, k = u // 2, u % 2
        sides(d, lambda zp: take(k, zp, d))

        @pl.when(u == 1)
        def _():
            for c in loads:
                c.wait()
            for i in range(1, n):
                meta_wait(i)

        sides(jnp.where(u == 1, 0, jnp.where((k == 0) & (d >= 2), d - 1, -1)), work)
        sides(jnp.where(k == 1, d - 1, -1), combine)
        return 0

    lax.fori_loop(0, 2 * zs + 2, step, 0)

    def relay(up, zp, c):
        chain_wait(up, zp, c)
        part[zp, c] = (part[zp, c].astype(F32) + chain[up, zp, c].astype(F32)).astype(BF16)
        chain_copy(zp, c).start()

    def hop(i, _):
        k, c = 1 + i // CHUNKS, i % CHUNKS
        down = zs - 1 - k

        def turn(t, _):
            up = jnp.where(z < zs // 2, 1 - t, t)

            @pl.when((up == 1) & (z > 0) & (z < k))
            def _():
                relay(1, k, c)

            @pl.when((up == 0) & (z < zs - 1) & (z > down))
            def _():
                relay(0, down, c)

            return 0

        return lax.fori_loop(0, 2, turn, 0)

    lax.fori_loop(0, (zs - 1) * CHUNKS, hop, 0)

    def pipe_copy(c):
        at = pl.ds(c * cols, cols)
        return remote(
            stage.at[c], out_ref.at[:, at], p_send.at[c], p_recv.at[c], pipe=prev_pipe
        )

    for c in range(CHUNKS):
        stage[c] = part[z, c]
        has_below, has_above = z > 0, z < zs - 1

        @pl.when(has_below & has_above)
        def _():
            chain_wait(1, z, c)
            chain_wait(0, z, c)
            stage[c] = (
                part[z, c].astype(F32) + chain[1, z, c].astype(F32) + chain[0, z, c].astype(F32)
            ).astype(BF16)

        @pl.when(has_below & (z == zs - 1))
        def _():
            chain_wait(1, z, c)
            stage[c] = (part[z, c].astype(F32) + chain[1, z, c].astype(F32)).astype(BF16)

        @pl.when(has_above & (z == 0))
        def _():
            chain_wait(0, z, c)
            stage[c] = (part[z, c].astype(F32) + chain[0, z, c].astype(F32)).astype(BF16)

        @pl.when(pipe > 0)
        def _():
            pipe_copy(c).start()

    for i in range(1, n):
        gg_wait(lax.rem(me + i, n))
    ggbuf[me] = ggout[me]
    total = ggbuf[0]
    for e in range(1, n):
        total = total + ggbuf[e]
    gg_ref[...] = total.astype(BF16)

    for k, p in pieces:
        @pl.when(z < zs - 1)
        def _():
            own_copy(k, p, 1).wait_send()

        @pl.when(z > 0)
        def _():
            own_copy(k, p, 0).wait_send()

    def drain(zp, _):
        @pl.when(can_fwd(zp))
        def _():
            for k, p in pieces:
                fwd_copy(k, p, zp).wait_send()

        for i in range(1, xs):
            for k, p in pieces:
                xsel_copy(k, p, zp, i).wait_send()

            def xcol(c, _):
                xret_copy(zp, c, i).wait_send()
                return 0

            lax.fori_loop(0, CHUNKS, xcol, 0)

        @pl.when(zp != z)
        def _():
            def ccol(c, _):
                chain_copy(zp, c).wait_send()
                return 0

            lax.fori_loop(0, CHUNKS, ccol, 0)

        return 0

    lax.fori_loop(0, zs, drain, 0)
    for i in range(1, n):
        meta_copy(i).wait_send()
        gg_copy(lax.rem(me + i, n)).wait_send()

    @pl.when(pipe > 0)
    def _():
        for c in range(CHUNKS):
            pipe_copy(c).wait_send()

    @pl.when(pipe < pipes - 1)
    def _():
        for c in range(CHUNKS):
            pipe_copy(c).wait_recv()

    @pl.when(pipe == pipes - 1)
    def _():
        out_ref[...] = jnp.zeros(out_ref.shape, BF16)


def local(pipes, tokens, out_grad, gates, expert_ids, w_gate, w_up, w_down):
    rows, width = tokens.shape[1:]
    top = expert_ids.shape[2]
    n = lax.axis_size("expert")
    xs = 1 << ((n.bit_length() - 1) // 2)
    zs = n // xs
    cap = max(2, 2 * rows * top // n)
    hidden = w_gate.shape[3]
    slots = xs * cap
    cols = width // CHUNKS
    span = width // PIECES
    dma = pltpu.SemaphoreType.DMA
    vmem = pl.BlockSpec(memory_space=pltpu.VMEM)
    hbm = pl.BlockSpec(memory_space=pl.ANY)
    arrived, gg = pl.pallas_call(
        functools.partial(kernel, pipes, zs, xs, cap),
        out_shape=(
            jax.ShapeDtypeStruct((rows, width), BF16),
            jax.ShapeDtypeStruct((top, rows), BF16),
        ),
        in_specs=[hbm, hbm, vmem, vmem, hbm, hbm, hbm],
        out_specs=(vmem, vmem),
        scratch_shapes=[
            pltpu.VMEM((width, hidden), BF16),
            pltpu.VMEM((width, hidden), BF16),
            pltpu.VMEM((hidden, width), BF16),
            pltpu.VMEM((2, PIECES, zs, rows, span), BF16),
            pltpu.VMEM((2, PIECES, zs, xs, cap, span), BF16),
            pltpu.VMEM((2, PIECES, zs, xs, cap, span), BF16),
            pltpu.VMEM((slots, hidden), F32),
            pltpu.VMEM((slots, hidden), F32),
            pltpu.VMEM((slots, hidden), BF16),
            pltpu.VMEM((slots, hidden), BF16),
            pltpu.VMEM((slots, 1), F32),
            pltpu.VMEM((zs, CHUNKS, xs, cap, cols), BF16),
            pltpu.VMEM((zs, CHUNKS, xs, cap, cols), BF16),
            pltpu.VMEM((zs, CHUNKS, rows, cols), BF16),
            pltpu.VMEM((2, zs, CHUNKS, rows, cols), BF16),
            pltpu.VMEM((CHUNKS, rows, cols), BF16),
            pltpu.VMEM((n, 8, rows), F32),
            pltpu.VMEM((n, top, rows), F32),
            pltpu.VMEM((n, top, rows), F32),
            dma((3,)),
            dma((2, PIECES)),
            dma((2, 2, PIECES)),
            dma((2, PIECES, zs)),
            dma((2, PIECES, zs)),
            dma((2, PIECES, zs, xs)),
            dma((2, PIECES, zs, xs)),
            dma((n,)),
            dma((n,)),
            dma((n,)),
            dma((n,)),
            dma((zs, CHUNKS, xs)),
            dma((zs, CHUNKS, xs)),
            dma((zs, CHUNKS)),
            dma((2, zs, CHUNKS)),
            dma((CHUNKS,)),
            dma((CHUNKS,)),
        ],
        compiler_params=pltpu.CompilerParams(
            collective_id=0, has_side_effects=True, vmem_limit_bytes=56 * 1024 * 1024
        ),
    )(
        tokens[0], out_grad[0], expert_ids[0].T, gates[0].T,
        w_gate[0, 0], w_up[0, 0], w_down[0, 0],
    )
    return arrived[None], gg.T[None]


def solution(mesh):
    row = P("pipe", "expert", None)
    weight = P("pipe", "expert", None, None)
    return jax.shard_map(
        functools.partial(local, mesh.shape["pipe"]),
        mesh=mesh,
        in_specs=(row, row, row, row, weight, weight, weight),
        out_specs=(row, row),
        check_vma=False,
    )
```
